32 devices in a mesh: ctx: 8 (over y, x, core), head: 4 (over z).
Axes of the slice: x: 2, y: 2, z: 4, core: 2. Of those that a mesh axis runs over, the one named last changes fastest.
Arguments:
- queries: bfloat16 [2048, 2048], P(('ctx', 'head')), may hold values from -6 to 6
- keys: bfloat16 [2048, 2048], P(('ctx', 'head')), may hold values from -6 to 6
- values: bfloat16 [2048, 2048], P(('ctx', 'head')), may hold values from -6 to 6
- ridge: float32 [16], P('head'), may hold values from 0.5 to 4
- gain: float32 [2048], P('head'), may hold values from 0.5 to 1.5
Outputs:
- mixed: bfloat16 [2048, 2048], P(('ctx', 'head'))
The draws below stay inside these ranges and needn't reach their ends.
All inputs are finite; a program needn't handle non-finite values.
Results may differ from the reference program's by a relative error of at most 0.0015.
Values may be sent and summed in bfloat16 or wider, within the bound.
A program may use at most 64 MiB of HBM per device.

```python
import math
import jax
import jax.numpy as jnp
from jax import lax

HEADS = 16
DH = 128
CTX_TOK = 256
ITERS = 4
TOKENS = 2048
N_CTX = 8


def draw_keys(key, part):
    base_key = jax.random.fold_in(key, 4711)
    noise_key, floor_key, mixing_key = jax.random.split(base_key, 3)
    floors = jnp.exp(jax.random.uniform(floor_key, (HEADS, 1), jnp.float32, math.log(0.003), math.log(0.03)))
    ladder = jnp.arange(DH, dtype=jnp.float32) / (DH - 1)
    spectrum = jnp.exp(ladder[None, :] * jnp.log(floors))
    mixing = jax.random.normal(mixing_key, (HEADS, DH, DH), jnp.float32) / math.sqrt(DH)
    source = jax.random.normal(noise_key, (TOKENS, HEADS, DH), jnp.float32)
    shaped = jnp.einsum('thd,hde->the', source * spectrum[None], mixing)
    shaped = shaped * lax_rsqrt_mean(spectrum)[None, :, None]
    shaped = jnp.clip(shaped, -6.0, 6.0)
    return shaped.reshape(TOKENS, HEADS * DH).astype(jnp.bfloat16)


def lax_rsqrt_mean(spectrum):
    return 1.0 / jnp.sqrt(jnp.mean(spectrum * spectrum, -1))


def block_levels(key, dims, cuts, smallest, high):
    loudness, own = 1.0, jax.random.fold_in(key, 6)
    for dim, parts in cuts:
        steps = jnp.exp(jax.random.uniform(jax.random.fold_in(own, dim), (parts,), jnp.float32, smallest / len(cuts), high / len(cuts)))
        loudness = loudness * jnp.repeat(steps, dims[dim] // parts).reshape([-1 if axis == dim else 1 for axis in range(len(dims))])
    return loudness


def scatter_about(stream_key, shape, scale, bound, cuts=(), held_as=jnp.bfloat16):
    entries = jax.random.normal(stream_key, shape, jnp.float32) * scale
    if len(cuts) > 0:
        entries = block_levels(stream_key, shape, cuts, -0.22, 0.18) * entries
    return jnp.clip(entries, min=-bound, max=bound).astype(held_as)


def setup_inputs(seed: int = 0) -> dict:
    key_list = jax.random.split(jax.random.key(seed), 6)
    return {
        "queries": scatter_about(key_list[0], (TOKENS, HEADS * DH), 1.0, 6.0, ((0, 32),)),
        "keys": draw_keys(jax.random.fold_in(key_list[5], 71), 0),
        "values": scatter_about(key_list[2], (TOKENS, HEADS * DH), 1.0, 6.0, ((0, 32),)),
        "ridge": jnp.clip(jnp.exp(math.log(4.0) - 2.0794415 * jax.random.uniform(key_list[3], (HEADS,), jnp.float32) ** block_levels(key_list[3], (HEADS,), ((0, 4),), -0.2, 0.2)), 0.5, 4.0),
        "gain": jnp.clip(1.0 + 0.1 * jax.random.normal(key_list[4], (HEADS * DH,), jnp.float32), 0.5, 1.5),
    }


EPS = 1e-06
HIGH = lax.Precision.HIGHEST

def unit_rows(matrix):
    return matrix * lax.rsqrt(lax.optimization_barrier(jnp.sum(matrix * matrix, -1, keepdims=True)) + EPS)

def solve_block(query_blk, key_blk, value_blk, key_state, value_state, strength):
    causal = jnp.tril(jnp.ones((CTX_TOK, CTX_TOK), jnp.float32))

    def apply_op(direction):
        scores = jnp.dot(direction, key_blk.T, precision=HIGH) * causal
        return jnp.dot(scores, key_blk, precision=HIGH) + jnp.dot(direction, key_state, precision=HIGH) + strength * direction
    answer = jnp.zeros_like(query_blk)
    resid = query_blk
    direction = query_blk
    rr_now = lax.optimization_barrier(jnp.sum(resid * resid, -1, keepdims=True))
    for turn in range(ITERS):
        image = apply_op(direction)
        alpha = rr_now / (lax.optimization_barrier(jnp.sum(direction * image, -1, keepdims=True)) + EPS)
        answer = answer + alpha * direction
        resid = resid - alpha * image
        rr_next = lax.optimization_barrier(jnp.sum(resid * resid, -1, keepdims=True))
        direction = resid + rr_next / (rr_now + EPS) * direction
        rr_now = rr_next
    scores = jnp.dot(answer, key_blk.T, precision=HIGH) * causal
    return jnp.dot(scores, value_blk, precision=HIGH) + jnp.dot(answer, value_state.T, precision=HIGH)

def reference(queries, keys, values, ridge, gain):

    def to_heads(matrix):
        return matrix.astype(jnp.float32).reshape(TOKENS, HEADS, DH).transpose(1, 0, 2).reshape(HEADS, N_CTX, CTX_TOK, DH)

    def one_head(items):
        query_h, key_h, value_h, strength = items
        query_h = unit_rows(query_h)
        key_h = unit_rows(key_h)

        def advance(carry, blocks):
            key_state, value_state = carry
            query_blk, key_blk, value_blk = blocks
            result = solve_block(query_blk, key_blk, value_blk, key_state, value_state, strength)
            key_state = key_state + jnp.dot(key_blk.T, key_blk, precision=HIGH)
            value_state = value_state + jnp.dot(value_blk.T, key_blk, precision=HIGH)
            return ((key_state, value_state), result)
        start = (jnp.zeros((DH, DH), jnp.float32), jnp.zeros((DH, DH), jnp.float32))
        carry_end, results = lax.scan(advance, start, (query_h, key_h, value_h))
        return results
    readout = lax.map(one_head, (to_heads(queries), to_heads(keys), to_heads(values), ridge))
    readout = readout.reshape(HEADS, TOKENS, DH)
    scale = lax.rsqrt(lax.optimization_barrier(jnp.mean(readout * readout, -1, keepdims=True)) + EPS)
    normed = readout * scale * gain.reshape(HEADS, 1, DH)
    return normed.transpose(1, 0, 2).reshape(TOKENS, HEADS * DH).astype(jnp.bfloat16)
```

```python
import functools

import jax
import jax.numpy as jnp
from jax import lax
from jax.experimental import pallas as pl
from jax.experimental.pallas import tpu as pltpu
from jax.sharding import PartitionSpec as P

ITERS = 4
EPS = 1e-06
CORES = 2
AHEAD = 3
VMEM_BYTES = 60 * 1024 * 1024
BF = jnp.bfloat16
F32 = jnp.float32
MESH = pl.DeviceIdType.MESH


def split(x):
    hi = x.astype(BF)
    return hi, (x - hi.astype(F32)).astype(BF)


def dot(a, b):
    return jnp.dot(a, b, preferred_element_type=F32)


def kernel(
    zn, chips, heads, width,
    q_ref, k_ref, v_ref, ridge_hbm, gain_hbm, out_ref,
    qbuf, kbuf, vbuf, obuf, ops, wmat, srow, xs, rs, ds, rrs,
    loc, tot, rbuf, pre, ridge_ref, gain_ref,
    in_send, in_recv, st_send, st_recv, out_send, out_recv, small,
):
    ctx = lax.axis_index("ctx")
    z = lax.axis_index("head")
    chip = ctx // CORES
    core = ctx % CORES
    group = CORES * zn
    rows = q_ref.shape[0]
    wide = heads * width
    span = zn * rows
    me = core * zn + z

    peers = []
    for dz in list(range(zn - 1, 0, -1)) + [0]:
        for dc in range(CORES):
            if dz or dc:
                pz = lax.rem(z + dz, zn)
                pc = lax.rem(core + dc, CORES)
                peers.append((pc, pz, pc * zn + pz, chip * CORES + pc))
    barrier = pltpu.get_barrier_semaphore()
    for pc, pz, pos, pctx in peers:
        pl.semaphore_signal(barrier, inc=1, device_id=(pctx, pz), device_id_type=MESH)
    for d in range(1, chips):
        other = lax.rem(chip + d, chips) * CORES + core
        pl.semaphore_signal(barrier, inc=1, device_id=(other, z), device_id_type=MESH)
    params = [
        pltpu.make_async_copy(ridge_hbm, ridge_ref, small.at[0]),
        pltpu.make_async_copy(gain_hbm, gain_ref, small.at[1]),
    ]
    for cp in params:
        cp.start()
    pl.semaphore_wait(barrier, len(peers) + chips - 1)

    def in_copy(i, src, dst, pos_from, pos_to, col_block, pctx, pz):
        h = i % heads
        return pltpu.make_async_remote_copy(
            src_ref=src.at[:, pl.ds(pl.multiple_of(col_block * wide + h * width, 128), width)],
            dst_ref=dst.at[h, pl.ds(pl.multiple_of(pos_from * rows, 16), rows), :],
            send_sem=in_send.at[i],
            recv_sem=in_recv.at[i],
            device_id=(pctx, pz),
            device_id_type=MESH,
        )

    streams = []
    for src, dst in ((k_ref, kbuf), (v_ref, vbuf), (q_ref, qbuf)):
        for h in range(heads):
            streams.append((len(streams), src, dst))
    def depart(i):
        _, src, dst = streams[i]
        h = i % heads
        pltpu.make_async_copy(
            src.at[:, pl.ds(pl.multiple_of((z * CORES + core) * wide + h * width, 128), width)],
            dst.at[h, pl.ds(pl.multiple_of(me * rows, 16), rows), :],
            in_recv.at[i],
        ).start()
        for pc, pz, pos, pctx in peers:
            in_copy(i, src, dst, me, pos, pz * CORES + pc, pctx, pz).start()

    for i in range(AHEAD):
        depart(i)

    def arrive(i):
        _, _, dst = streams[i]
        whole = dst.at[i % heads]
        pltpu.make_async_copy(whole, whole, in_recv.at[i]).wait()
        if i + AHEAD < len(streams):
            depart(i + AHEAD)

    def st_copy(d, i):
        return pltpu.make_async_remote_copy(
            src_ref=tot.at[i],
            dst_ref=rbuf.at[d - 1, i],
            send_sem=st_send.at[d - 1, i],
            recv_sem=st_recv.at[d - 1, i],
            device_id=(lax.rem(chip + d, chips) * CORES + core, z),
            device_id_type=MESH,
        )

    half = span // 2
    chunks = [slice(j * span, (j + 1) * span) for j in range(CORES)]

    def offer(h, base):
        i = base + h
        tot[i] = loc[i, 0] + loc[i, 1]
        pre[i] = jnp.zeros((width, width), F32)
        for d in range(1, chips):
            @pl.when(chip + d < chips)
            def _():
                st_copy(d, i).start()

    def collect(h, base):
        i = base + h
        for d in range(1, chips):
            @pl.when(chip >= d)
            def _():
                st_copy(d, i).wait_recv()
                pre[i] = pre[i] + rbuf[d - 1, i]

    causal = (
        lax.broadcasted_iota(jnp.int32, (span, span), 1)
        <= lax.broadcasted_iota(jnp.int32, (span, span), 0)
    )

    def fill(n, at, block):
        ops[n, :width, at:at + block.shape[1]] = block
        ops[n, width:, at:at + block.shape[1]] = block

    for h in range(heads):
        arrive(h)
        for j, r in enumerate(chunks):
            n = h * CORES + j
            key = kbuf[h, r]
            key_t = key.astype(F32).T
            s = lax.rsqrt(jnp.sum(key_t * key_t, 0, keepdims=True) + EPS)
            srow[n] = jnp.broadcast_to(s, (8, span))
            fill(n, 0, key_t.astype(BF))
            hi, lo = split(key_t * (s * s))
            loc[h, j] = dot(hi, key) + dot(lo, key)
        offer(h, 0)
    for n in range(heads * CORES):
        s = srow[n][0:1]
        wmat[n] = jnp.where(causal, s * s, 0.0)

    for h in range(heads):
        arrive(heads + h)
        for j, r in enumerate(chunks):
            n = h * CORES + j
            key_t = ops[n, :width, :span].astype(F32)
            hi, lo = split(key_t * srow[n][0:1])
            val = vbuf[h, r]
            loc[heads + h, j] = dot(hi, val) + dot(lo, val)
        offer(h, heads)

    def states(h, base):
        for j in range(CORES):
            state = pre[base + h]
            if j:
                state = state + loc[base + h, 0]
            hi, lo = split(state)
            fill(h * CORES + j, span, hi)
            fill(h * CORES + j, span + width, lo)

    for h in range(heads):
        collect(h, 0)
        states(h, 0)
    for cp in params:
        cp.wait()

    def products(n, d, weights, right):
        both = dot(jnp.concatenate(split(d), 1), ops[n])
        left = jnp.concatenate(split(both[:, :half] * weights[:, :half]), 1)
        low = jnp.concatenate(split(both[half:, half:span] * weights[half:, half:]), 1)
        first, second = right[:half], right[half:]
        image = dot(left, jnp.concatenate([first, first], 0))
        lower = image[half:] + dot(low, jnp.concatenate([second, second], 0))
        return (
            jnp.concatenate([image[:half], lower], 0)
            + both[:, span:span + width] + both[:, span + width:]
        )

    def turns(h, start, stop):
        strength = ridge_ref[core * heads + h]

        def turn(_, carry):
            for j, r in enumerate(chunks):
                n = h * CORES + j
                d = ds[n]
                rr = rrs[n]
                image = products(n, d, wmat[n], kbuf[h, r]) + strength * d
                alpha = rr / (jnp.broadcast_to(jnp.sum(d * image, -1, keepdims=True), d.shape) + EPS)
                xs[n] = xs[n] + alpha * d
                res = rs[n] - alpha * image
                rs[n] = res
                nxt = jnp.broadcast_to(jnp.sum(res * res, -1, keepdims=True), res.shape)
                ds[n] = res + nxt / (rr + EPS) * d
                rrs[n] = nxt
            return carry

        lax.fori_loop(start, stop, turn, 0)

    def out_copy(h, pos_to, pos_from, zf, cf, pctx, pz):
        cols = pl.ds(pl.multiple_of((zf * CORES + cf) * wide + h * width, 128), width)
        return pltpu.make_async_remote_copy(
            src_ref=obuf.at[h, pl.ds(pl.multiple_of(pos_to * rows, 16), rows), :],
            dst_ref=out_ref.at[:, cols],
            send_sem=out_send.at[h],
            recv_sem=out_recv.at[h],
            device_id=(pctx, pz),
            device_id_type=MESH,
        )

    for h in range(heads):
        arrive(2 * heads + h)
        for j, r in enumerate(chunks):
            n = h * CORES + j
            qry = qbuf[h, r].astype(F32)
            qn = qry * lax.rsqrt(jnp.sum(qry * qry, -1, keepdims=True) + EPS)
            rs[n] = qn
            ds[n] = qn
            xs[n] = jnp.zeros((span, width), F32)
            rrs[n] = jnp.broadcast_to(jnp.sum(qn * qn, -1, keepdims=True), qn.shape)
        turns(h, 0, ITERS)
        collect(h, heads)
        states(h, heads)
        for j, r in enumerate(chunks):
            n = h * CORES + j
            weights = jnp.where(causal, srow[n][0:1], 0.0)
            read = products(n, xs[n], weights, vbuf[h, r])
            scale = lax.rsqrt(jnp.mean(read * read, -1, keepdims=True) + EPS)
            g = gain_ref[pl.ds(pl.multiple_of(core * wide + h * width, 128), width)]
            obuf[h, r] = (read * scale * g[None, :]).astype(BF)
            for dz in range(zn - 1, 0, -1):
                pz = lax.rem(z + dz, zn)
                out_copy(h, j * zn + pz, me, z, core, chip * CORES + j, pz).start()

            @pl.when(core != j)
            def _():
                out_copy(h, j * zn + z, me, z, core, chip * CORES + j, z).start()

    for h in range(heads):
        mine = pl.ds(pl.multiple_of((z * CORES + core) * wide + h * width, 128), width)
        out_ref[:, mine] = obuf[h, pl.ds(pl.multiple_of(me * rows, 16), rows), :]
    for h in range(heads):
        got = obuf.at[h, pl.ds(0, (group - 1) * rows), :]
        pltpu.make_async_copy(got, got, out_recv.at[h]).wait()
    for i, src, dst in streams:
        sent = dst.at[i % heads, pl.ds(0, (group - 1) * rows), :]
        pltpu.make_async_copy(sent, sent, in_send.at[i]).wait()
    for i in range(2 * heads):
        for d in range(1, chips):
            @pl.when(chip + d < chips)
            def _():
                st_copy(d, i).wait_send()
    for h in range(heads):
        sent = obuf.at[h, pl.ds(0, (group - 1) * rows), :]
        pltpu.make_async_copy(sent, sent, out_send.at[h]).wait()


def solution(mesh):
    zn = mesh.shape["head"]
    chips = mesh.shape["ctx"] // CORES

    def on_device(queries, keys, values, ridge, gain):
        rows, cols = queries.shape
        local = ridge.shape[0]
        width = gain.shape[0] // local
        heads = local // CORES
        wide = heads * width
        span = zn * rows
        group = CORES * zn
        count = heads * CORES
        vm = pltpu.VMEM
        dma = pltpu.SemaphoreType.DMA
        any_spec = pl.BlockSpec(memory_space=pltpu.HBM)
        return pl.pallas_call(
            functools.partial(kernel, zn, chips, heads, width),
            out_shape=pltpu.VMEM((rows, cols), BF),
            in_specs=[
                any_spec, any_spec, any_spec, any_spec, any_spec,
            ],
            out_specs=pl.BlockSpec(memory_space=pltpu.VMEM),
            scratch_shapes=[
                vm((heads, CORES * span, width), BF),
                vm((heads, CORES * span, width), BF),
                vm((heads, CORES * span, width), BF),
                vm((heads, CORES * span, width), BF),
                vm((count, 2 * width, span + 2 * width), BF),
                vm((count, span, span), F32),
                vm((count, 8, span), F32),
                vm((count, span, width), F32),
                vm((count, span, width), F32),
                vm((count, span, width), F32),
                vm((count, span, width), F32),
                vm((2 * heads, CORES, width, width), F32),
                vm((2 * heads, width, width), F32),
                vm((max(chips - 1, 1), 2 * heads, width, width), F32),
                vm((2 * heads, width, width), F32),
                pltpu.SMEM((local,), F32),
                vm((local * width,), F32),
                dma((3 * heads,)), dma((3 * heads,)),
                dma((max(chips - 1, 1), 2 * heads)), dma((max(chips - 1, 1), 2 * heads)),
                dma((heads,)), dma((heads,)), dma((2,)),
            ],
            compiler_params=pltpu.CompilerParams(
                collective_id=0, has_side_effects=True,
                vmem_limit_bytes=VMEM_BYTES - rows * cols * 2,
            ),
            name="mesa",
        )(queries, keys, values, ridge, gain)

    tokens = P(("ctx", "head"), None)
    return jax.shard_map(
        on_device, mesh=mesh,
        in_specs=(tokens, tokens, tokens, P("head"), P("head")),
        out_specs=tokens, check_vma=False,
    )
```

```python
import functools

import jax
import jax.numpy as jnp
from jax import lax
from jax.experimental import pallas as pl
from jax.experimental.pallas import tpu as pltpu
from jax.sharding import PartitionSpec as P

ITERS = 4
EPS = 1e-06
CORES = 2
AHEAD = 3
AT = 2
VMEM_BYTES = 60 * 1024 * 1024
BF = jnp.bfloat16
F32 = jnp.float32
MESH = pl.DeviceIdType.MESH


def split(x):
    hi = x.astype(BF)
    return hi, (x - hi.astype(F32)).astype(BF)


def dot(a, b):
    return jnp.dot(a, b, preferred_element_type=F32)


def kernel(
    zn, chips, heads, width,
    q_ref, k_ref, v_ref, ridge_hbm, gain_hbm, out_ref,
    qbuf, kbuf, vbuf, obuf, ops, wmat, srow, xs, rs, ds, rrs, ims,
    loc, tot, rbuf, pre, ridge_ref, gain_ref,
    in_send, in_recv, st_send, st_recv, out_send, out_recv, small,
):
    ctx = lax.axis_index("ctx")
    z = lax.axis_index("head")
    chip = ctx // CORES
    core = ctx % CORES
    group = CORES * zn
    rows = q_ref.shape[0]
    wide = heads * width
    span = zn * rows
    me = core * zn + z

    low = (z < zn // 2).astype(jnp.int32)
    peers = []
    for rr in range(zn - 1):
        r = lax.rem(rr + core * (zn - 2), zn - 1)
        down = zn - 1 - r - (zn - 1 - r <= z).astype(jnp.int32)
        up = r + (r >= z).astype(jnp.int32)
        pz = low * down + (1 - low) * up
        for dc in range(CORES):
            pc = lax.rem(core + dc, CORES)
            peers.append((pc, pz, pc * zn + pz, chip * CORES + pc))
    pc = lax.rem(core + 1, CORES)
    peers.append((pc, z, pc * zn + z, chip * CORES + pc))

    barrier = pltpu.get_barrier_semaphore()
    for pc, pz, pos, pctx in peers:
        pl.semaphore_signal(barrier, inc=1, device_id=(pctx, pz), device_id_type=MESH)
    for d in range(1, chips):
        other = lax.rem(chip + d, chips) * CORES + core
        pl.semaphore_signal(barrier, inc=1, device_id=(other, z), device_id_type=MESH)
    params = [
        pltpu.make_async_copy(ridge_hbm, ridge_ref, small.at[0]),
        pltpu.make_async_copy(gain_hbm, gain_ref, small.at[1]),
    ]
    for cp in params:
        cp.start()
    pl.semaphore_wait(barrier, len(peers) + chips - 1)

    def in_copy(i, src, dst, h, pos_from, pos_to, col_block, pctx, pz):
        return pltpu.make_async_remote_copy(
            src_ref=src.at[:, pl.ds(pl.multiple_of(col_block * wide + h * width, 128), width)],
            dst_ref=dst.at[h, pl.ds(pl.multiple_of(pos_from * rows, 16), rows), :],
            send_sem=in_send.at[i],
            recv_sem=in_recv.at[i],
            device_id=(pctx, pz),
            device_id_type=MESH,
        )

    keys = [("k", h) for h in range(heads)]
    values = [("v", h) for h in range(heads)]
    queries = [("q", h) for h in range(heads)]
    sources = {"k": (k_ref, kbuf), "v": (v_ref, vbuf), "q": (q_ref, qbuf)}
    streams = keys + [x for h in range(heads) for x in (values[h], queries[h])]

    def depart(i):
        kind, h = streams[i]
        src, dst = sources[kind]
        pltpu.make_async_copy(
            src.at[:, pl.ds(pl.multiple_of((z * CORES + core) * wide + h * width, 128), width)],
            dst.at[h, pl.ds(pl.multiple_of(me * rows, 16), rows), :],
            in_recv.at[i],
        ).start()
        for pc, pz, pos, pctx in peers:
            in_copy(i, src, dst, h, me, pos, pz * CORES + pc, pctx, pz).start()

    for i in range(AHEAD):
        depart(i)

    def arrive(item):
        i = streams.index(item)
        whole = sources[item[0]][1].at[item[1]]
        pltpu.make_async_copy(whole, whole, in_recv.at[i]).wait()
        if i + AHEAD < len(streams):
            depart(i + AHEAD)

    def st_copy(d, i):
        return pltpu.make_async_remote_copy(
            src_ref=tot.at[i],
            dst_ref=rbuf.at[d - 1, i],
            send_sem=st_send.at[d - 1, i],
            recv_sem=st_recv.at[d - 1, i],
            device_id=(lax.rem(chip + d, chips) * CORES + core, z),
            device_id_type=MESH,
        )

    half = span // 2
    chunks = [slice(j * span, (j + 1) * span) for j in range(CORES)]

    def offer(h, base):
        i = base + h
        tot[i] = loc[i, 0] + loc[i, 1]
        pre[i] = jnp.zeros((width, width), F32)
        for d in range(1, chips):
            @pl.when(chip + d < chips)
            def _():
                st_copy(d, i).start()

    def collect(h, base):
        i = base + h
        for d in range(1, chips):
            @pl.when(chip >= d)
            def _():
                st_copy(d, i).wait_recv()
                pre[i] = pre[i] + rbuf[d - 1, i]

    causal = (
        lax.broadcasted_iota(jnp.int32, (span, span), 1)
        <= lax.broadcasted_iota(jnp.int32, (span, span), 0)
    )

    def fill(n, at, block):
        ops[n, :width, at:at + block.shape[1]] = block
        ops[n, width:, at:at + block.shape[1]] = block

    for h in range(heads):
        arrive(keys[h])
        for j, r in enumerate(chunks):
            n = h * CORES + j
            key = kbuf[h, r]
            key_t = key.astype(F32).T
            s = lax.rsqrt(jnp.sum(key_t * key_t, 0, keepdims=True) + EPS)
            srow[n] = jnp.broadcast_to(s, (8, span))
            fill(n, 0, key_t.astype(BF))
            hi, lo = split(key_t * (s * s))
            loc[h, j] = dot(hi, key) + dot(lo, key)
        offer(h, 0)
    for n in range(heads * CORES):
        s = srow[n][0:1]
        wmat[n] = jnp.where(causal, s * s, 0.0)

    eye = jnp.where(
        lax.broadcasted_iota(jnp.int32, (width, width), 0)
        == lax.broadcasted_iota(jnp.int32, (width, width), 1),
        1.0, 0.0,
    ).astype(F32)

    def states(h, base):
        for j in range(CORES):
            state = pre[base + h]
            if not base:
                state = state + ridge_ref[core * heads + h] * eye
            if j:
                state = state + loc[base + h, 0]
            hi, lo = split(state)
            fill(h * CORES + j, span, hi)
            fill(h * CORES + j, span + width, lo)

    def products(n, d, weights, right):
        both = dot(jnp.concatenate(split(d), 1), ops[n])
        left = jnp.concatenate(split(both[:, :half] * weights[:, :half]), 1)
        low = jnp.concatenate(split(both[half:, half:span] * weights[half:, half:]), 1)
        first, second = right[:half], right[half:]
        image = dot(left, jnp.concatenate([first, first], 0))
        lower = image[half:] + dot(low, jnp.concatenate([second, second], 0))
        return (
            jnp.concatenate([image[:half], lower], 0)
            + both[:, span:span + width] + both[:, span + width:]
        )

    def spread(x):
        return jnp.broadcast_to(jnp.sum(x, -1, keepdims=True), x.shape)

    def apply(h, j):
        n = h * CORES + j
        ims[n] = products(n, ds[n], wmat[n], kbuf[h, chunks[j]])

    def update(h, j, turn):
        n = h * CORES + j
        d = ds[n]
        rr = rrs[n]
        image = ims[n]
        alpha = rr / (spread(d * image) + EPS)
        xs[n] = alpha * d if turn == 0 else xs[n] + alpha * d
        if turn == ITERS - 1:
            return
        res = rs[n] - alpha * image
        rs[n] = res
        nxt = spread(res * res)
        ds[n] = res + nxt / (rr + EPS) * d
        rrs[n] = nxt

    def begin(h):
        for j, r in enumerate(chunks):
            n = h * CORES + j
            qry = qbuf[h, r].astype(F32)
            qn = qry * lax.rsqrt(jnp.sum(qry * qry, -1, keepdims=True) + EPS)
            rs[n] = qn
            ds[n] = qn
            rrs[n] = spread(qn * qn)
        collect(h, 0)
        states(h, 0)
        apply(h, 0)

    def advance(h, turn):
        update(h, 0, turn)
        apply(h, 1)
        if turn < ITERS - 1:
            apply(h, 0)
        update(h, 1, turn)

    def out_copy(h, pos_to, pos_from, zf, cf, pctx, pz):
        cols = pl.ds(pl.multiple_of((zf * CORES + cf) * wide + h * width, 128), width)
        return pltpu.make_async_remote_copy(
            src_ref=obuf.at[h, pl.ds(pl.multiple_of(pos_to * rows, 16), rows), :],
            dst_ref=out_ref.at[:, cols],
            send_sem=out_send.at[h],
            recv_sem=out_recv.at[h],
            device_id=(pctx, pz),
            device_id_type=MESH,
        )

    def readout(h):
        collect(h, heads)
        states(h, heads)
        for j, r in enumerate(chunks):
            n = h * CORES + j
            weights = jnp.where(causal, srow[n][0:1], 0.0)
            read = products(n, xs[n], weights, vbuf[h, r])
            scale = lax.rsqrt(jnp.mean(read * read, -1, keepdims=True) + EPS)
            g = gain_ref[pl.ds(pl.multiple_of(core * wide + h * width, 128), width)]
            obuf[h, r] = (read * scale * g[None, :]).astype(BF)
            for _, pz, _, _ in peers[:-1:CORES]:
                out_copy(h, j * zn + pz, me, z, core, chip * CORES + j, pz).start()

            @pl.when(core != j)
            def _():
                out_copy(h, j * zn + z, me, z, core, chip * CORES + j, z).start()

    for cp in params:
        cp.wait()
    def value_state(h):
        arrive(values[h])
        for j, r in enumerate(chunks):
            n = h * CORES + j
            key_t = ops[n, :width, :span].astype(F32)
            hi, lo = split(key_t * srow[n][0:1])
            val = vbuf[h, r]
            loc[heads + h, j] = dot(hi, val) + dot(lo, val)
        offer(h, heads)

    def solve(h, middle):
        arrive(queries[h])
        begin(h)
        for turn in range(ITERS):
            advance(h, turn)
            if turn == AT:
                middle()

    value_state(0)
    for h in range(heads):
        solve(h, lambda: None)
        if h + 1 < heads:
            value_state(h + 1)
        readout(h)

    for h in range(heads):
        mine = pl.ds(pl.multiple_of((z * CORES + core) * wide + h * width, 128), width)
        out_ref[:, mine] = obuf[h, pl.ds(pl.multiple_of(me * rows, 16), rows), :]
    for h in range(heads):
        got = obuf.at[h, pl.ds(0, (group - 1) * rows), :]
        pltpu.make_async_copy(got, got, out_recv.at[h]).wait()
    for i, (kind, h) in enumerate(streams):
        sent = sources[kind][1].at[h, pl.ds(0, (group - 1) * rows), :]
        pltpu.make_async_copy(sent, sent, in_send.at[i]).wait()
    for i in range(2 * heads):
        for d in range(1, chips):
            @pl.when(chip + d < chips)
            def _():
                st_copy(d, i).wait_send()
    for h in range(heads):
        sent = obuf.at[h, pl.ds(0, (group - 1) * rows), :]
        pltpu.make_async_copy(sent, sent, out_send.at[h]).wait()


def solution(mesh):
    zn = mesh.shape["head"]
    chips = mesh.shape["ctx"] // CORES

    def on_device(queries, keys, values, ridge, gain):
        rows, cols = queries.shape
        local = ridge.shape[0]
        width = gain.shape[0] // local
        heads = local // CORES
        wide = heads * width
        span = zn * rows
        group = CORES * zn
        count = heads * CORES
        vm = pltpu.VMEM
        dma = pltpu.SemaphoreType.DMA
        any_spec = pl.BlockSpec(memory_space=pltpu.HBM)
        return pl.pallas_call(
            functools.partial(kernel, zn, chips, heads, width),
            out_shape=pltpu.VMEM((rows, cols), BF),
            in_specs=[
                any_spec, any_spec, any_spec, any_spec, any_spec,
            ],
            out_specs=pl.BlockSpec(memory_space=pltpu.VMEM),
            scratch_shapes=[
                vm((heads, CORES * span, width), BF),
                vm((heads, CORES * span, width), BF),
                vm((heads, CORES * span, width), BF),
                vm((heads, CORES * span, width), BF),
                vm((count, 2 * width, span + 2 * width), BF),
                vm((count, span, span), F32),
                vm((count, 8, span), F32),
                vm((count, span, width), F32),
                vm((count, span, width), F32),
                vm((count, span, width), F32),
                vm((count, span, width), F32),
                vm((count, span, width), F32),
                vm((2 * heads, CORES, width, width), F32),
                vm((2 * heads, width, width), F32),
                vm((max(chips - 1, 1), 2 * heads, width, width), F32),
                vm((2 * heads, width, width), F32),
                pltpu.SMEM((local,), F32),
                vm((local * width,), F32),
                dma((3 * heads,)), dma((3 * heads,)),
                dma((max(chips - 1, 1), 2 * heads)), dma((max(chips - 1, 1), 2 * heads)),
                dma((heads,)), dma((heads,)), dma((2,)),
            ],
            compiler_params=pltpu.CompilerParams(
                collective_id=0, has_side_effects=True,
                vmem_limit_bytes=VMEM_BYTES - rows * cols * 2,
            ),
            name="mesa",
        )(queries, keys, values, ridge, gain)

    tokens = P(("ctx", "head"), None)
    return jax.shard_map(
        on_device, mesh=mesh,
        in_specs=(tokens, tokens, tokens, P("head"), P("head")),
        out_specs=tokens, check_vma=False,
    )
```
